32 devices in a mesh: grp: 8 (over z, x), row: 4 (over y, core).
Axes of the slice: x: 2, y: 2, z: 4, core: 2. Of those that a mesh axis runs over, the one named last changes fastest.
Arguments:
- couplings: bfloat16 [8, 288, 6016], P('grp', 'row'), may hold values from -0.078125 to 0.078125
- ell_scale: float32 [6016], replicated, may hold values from 0.5 to 2
- bin_weight: float32 [128], replicated, may hold values from 0.3 to 1.5
- bin_edges: int32 [129], replicated, may hold values from 0 to 6016, as said below
- pair_table: int32 [8], replicated, may hold values from 0 to 7, as said below
Outputs:
- covariance: float32 [8, 288, 288], P('grp', 'row')
The draws below stay inside these ranges and needn't reach their ends.
Inputs may be any that keep to these rules, and one draw needn't show every extreme that they name: Strictly increasing, bin_edges[0] = 0 and bin_edges[128] = 6016. `pair_table`: each coupling matrix is the second of exactly one pair.
All inputs are finite; a program needn't handle non-finite values.
Results may differ from the reference program's by a relative error of at most 0.0056.
Values may be sent and summed in bfloat16 or wider, within the bound.
No kernel may reach another device: no remote copies, remote signals or barrier semaphores. Data moves between devices by JAX's collectives and lax.ppermute only.
A program may use at most 128 MiB of HBM per device.

```python
import math
import jax
import jax.numpy as jnp
from jax import lax

L = 6016
NBIN = 128
NCOUP = 8
W = 288


def draw_bin_edges(key, part):
    order = jax.random.permutation(jax.random.fold_in(key, 17), L - 1) + 1
    cuts = jnp.sort(order[:NBIN - 1]).astype(jnp.int32)
    return jnp.concatenate([jnp.zeros((1,), jnp.int32), cuts, jnp.full((1,), L, jnp.int32)])


def draw_pair_table(key, part):
    perm = jax.random.permutation(jax.random.fold_in(key, 29), NCOUP).astype(jnp.int32)
    first = jax.random.randint(jax.random.fold_in(key, 31), (), 0, NCOUP).astype(jnp.int32)
    target = ((first + NCOUP // 2) % NCOUP).astype(jnp.int32)
    where_target = jnp.argmax((perm == target).astype(jnp.int32)).astype(jnp.int32)
    held = perm[first]
    perm = perm.at[where_target].set(held)
    perm = perm.at[first].set(target)
    return perm.astype(jnp.int32)


def block_levels(key, shape, split, low, high):
    def one(dim, parts):
        draws = jax.random.uniform(jax.random.fold_in(jax.random.fold_in(key, 6), dim), (parts,), jnp.float32, low / len(split), high / len(split))
        return jnp.repeat(jnp.exp(draws), shape[dim] // parts).reshape((-1,) + (1,) * (len(shape) - dim - 1))

    level = one(*split[0])
    for cut in split[1:]:
        level = level * one(*cut)
    return level


def scatter_about(rng, shape, spread, most, cuts=(), held_as=jnp.bfloat16):
    drawn = jax.random.normal(rng, shape, jnp.float32) * spread
    if len(cuts) > 0:
        drawn = block_levels(rng, shape, cuts, -0.22, 0.18) * drawn
    return jnp.clip(drawn, min=-most, max=most).astype(held_as)


def setup_inputs(seed: int = 0) -> dict:
    key_list = jax.random.split(jax.random.key(seed), 6)
    return {
        "couplings": scatter_about(key_list[0], (NCOUP, W, L), L ** -0.5, 0.078125, ((0, 8), (1, 4))),
        "ell_scale": jnp.clip(jnp.exp(jax.random.uniform(key_list[1], (L,), jnp.float32, math.log(0.5), math.log(2.0))), 0.5, 2.0),
        "bin_weight": jnp.clip(jnp.exp(jax.random.uniform(key_list[2], (NBIN,), jnp.float32, math.log(0.3), math.log(1.5))), 0.3, 1.5),
        "bin_edges": draw_bin_edges(jax.random.fold_in(key_list[5], 71), 0),
        "pair_table": draw_pair_table(jax.random.fold_in(key_list[5], 71), 0),
    }


def bin_matrix(bin_edges, width):
    ell = jnp.arange(width, dtype=jnp.int32)[:, None]
    inside = (ell >= bin_edges[None, :-1]) & (ell < bin_edges[None, 1:])
    return inside.astype(jnp.bfloat16)


def factor_rows(coupling, ell_scale, bin_weight, table):
    weighted = (coupling.astype(jnp.float32) * ell_scale[None, :]).astype(jnp.bfloat16)
    binned = jnp.dot(weighted, table, preferred_element_type=jnp.float32)
    binned = (binned * bin_weight[None, :]).astype(jnp.bfloat16)
    return jnp.concatenate([weighted, binned], axis=1)


def reference(couplings, ell_scale, bin_weight, bin_edges, pair_table):
    table = bin_matrix(bin_edges, L)

    def build(coupling):
        return factor_rows(coupling, ell_scale, bin_weight, table)

    factors_all = lax.map(build, couplings)

    def product(args):
        own, partner = args
        other = factors_all[partner]
        return jnp.dot(own, other.T, preferred_element_type=jnp.float32)

    return lax.map(product, (factors_all, pair_table.astype(jnp.int32)))
```

```python
import functools

import jax
import jax.numpy as jnp
from jax import lax
from jax.experimental import pallas as pl
from jax.experimental.pallas import tpu as pltpu
from jax.sharding import PartitionSpec as P


LANES = 128
WIRE = jnp.bfloat16
CONTRACT_LAST = (((1,), (1,)), ((), ()))
VMEM = pl.BlockSpec(memory_space=pltpu.VMEM)
SMEM = pl.BlockSpec(memory_space=pltpu.SMEM)


def basis_of(count):
    bits = count.bit_length() - 1
    return [(1 << b) | ((1 << (b - 1)) if b >= 2 else 0) for b in range(bits)]


def slot_of(coordinate, basis):
    slot = 0
    for b, generator in enumerate(basis):
        if coordinate >> (len(basis) - 1 - b) & 1:
            slot ^= generator
    return slot


def swap(x, axis, size, generator):
    return lax.ppermute(x, axis, [(i, i ^ generator) for i in range(size)])


def prepare_kernel(count, width, pos, coupling, scale, weight, low, high, keep, send):
    group, core = pos[0], pos[1]
    rows, columns = coupling.shape
    bins = low.shape[1]
    binned = jnp.zeros((rows, bins), jnp.float32)
    for j in range(2 * count):
        first, last = j * width, (j + 1) * width
        parts = []
        raw = max(0, min(last, columns) - first)
        if raw:
            span = slice(first, first + raw)
            part = (coupling[:, span].astype(jnp.float32) * scale[:, span]).astype(jnp.bfloat16)
            ell = first + lax.broadcasted_iota(jnp.int32, (raw, bins), 0)
            inside = (ell >= low[...]) & (ell < high[...])
            table = jnp.where(inside, 1.0, 0.0).astype(jnp.bfloat16)
            binned += jnp.dot(part, table, preferred_element_type=jnp.float32)
            parts.append(part)
        if first < columns + bins and last > columns:
            tail = (binned * weight[...]).astype(jnp.bfloat16)
            parts.append(tail[:, max(0, first - columns) : min(bins, last - columns)])
        filled = sum(p.shape[1] for p in parts)
        if filled < width:
            parts.append(jnp.zeros((rows, width - filled), jnp.bfloat16))
        chunk = parts[0] if len(parts) == 1 else jnp.concatenate(parts, axis=1)
        slot = (j % count) ^ group

        @pl.when(core == j // count)
        def _():
            keep[slot] = chunk

        @pl.when(core != j // count)
        def _():
            send[slot] = chunk


def assemble_kernel(count, keep, received, *slots):
    rows = keep.shape[1]
    for d in range(count):
        slots[d][:rows] = keep[d]
        slots[d][rows:] = received[d]


def product_kernel(count, basis, pos, pair, *refs):
    lefts, rights = refs[:count], refs[count : 2 * count]
    keep, send, held = refs[2 * count :]
    group = pos[0]
    rows = keep.shape[1]
    for d in range(count):
        held[d] = rights[d][...]
    for k in range(count):
        d = slot_of(k, basis)
        partner = pair[d ^ group] ^ group
        block = lax.dot_general(
            lefts[d][...], held[partner], CONTRACT_LAST, preferred_element_type=jnp.float32
        )
        keep[k] = block[:rows]
        other = block[rows:]
        send[k] = jnp.concatenate([other[:, rows:], other[:, :rows]], axis=1).astype(send.dtype)


def finish_kernel(count, pos, *refs):
    kept, received, out = refs[:count], refs[count : 2 * count], refs[2 * count]
    held = refs[2 * count + 1]
    block, core = pos[2], pos[1]
    rows = out.shape[0]
    for e in range(count):
        total = kept[e][0] + received[e][0].astype(jnp.float32)
        held[2 * e] = total[:, :rows]
        held[2 * e + 1] = total[:, rows:]
    for h in range(count):
        for c in range(2):
            at = (2 * h + c) * rows
            out[:, at : at + rows] = held[2 * (block ^ h) + (core ^ c)]


def body(groups, row_devices, couplings, ell_scale, bin_weight, bin_edges, pair_table):
    coupling = couplings[0]
    rows, columns = coupling.shape
    bins = bin_weight.shape[0]
    group, row = lax.axis_index("grp"), lax.axis_index("row")
    pos = jnp.stack([group, row % 2, row // 2]).astype(jnp.int32)
    width = LANES * pl.cdiv(columns + bins, LANES * 2 * groups)
    basis = basis_of(groups)
    blocks = row_devices // 2

    half = jax.ShapeDtypeStruct((groups, rows, width), jnp.bfloat16)
    keep, send = pl.pallas_call(
        functools.partial(prepare_kernel, groups, width),
        out_shape=(half, half),
        in_specs=[SMEM] + [VMEM] * 5,
        out_specs=(VMEM, VMEM),
    )(pos, coupling, ell_scale[None], bin_weight[None], bin_edges[None, :-1], bin_edges[None, 1:])
    received = swap(send, "row", row_devices, 1)
    mine = pl.pallas_call(
        functools.partial(assemble_kernel, groups),
        out_shape=[jax.ShapeDtypeStruct((2 * rows, width), jnp.bfloat16)] * groups,
        in_specs=[VMEM] * 2,
        out_specs=[VMEM] * groups,
    )(keep, received)
    held = [mine[0]] + [swap(mine[d], "grp", groups, d) for d in range(1, groups)]

    def products(rights):
        shape = (groups, rows, 2 * rows)
        kept, sent = pl.pallas_call(
            functools.partial(product_kernel, groups, basis),
            out_shape=(jax.ShapeDtypeStruct(shape, jnp.float32), jax.ShapeDtypeStruct(shape, WIRE)),
            in_specs=[SMEM] * 2 + [VMEM] * (2 * groups),
            out_specs=(VMEM, VMEM),
            scratch_shapes=[pltpu.VMEM((groups, 2 * rows, width), jnp.bfloat16)],
        )(pos, pair_table, *held, *rights)
        other = swap(sent, "row", row_devices, 1)
        for generator in basis:
            total = kept + other.astype(jnp.float32)
            middle = total.shape[0] // 2
            kept = total[:middle]
            other = swap(total[middle:].astype(WIRE), "grp", groups, generator)
        return kept, other

    parts = []
    for e in range(blocks):
        rights = held if e == 0 else [swap(x, "row", row_devices, 2 * e) for x in held]
        parts.append(products(rights))
    return pl.pallas_call(
        functools.partial(finish_kernel, blocks),
        out_shape=jax.ShapeDtypeStruct((rows, row_devices * rows), jnp.float32),
        in_specs=[SMEM] + [VMEM] * (2 * blocks),
        out_specs=VMEM,
        scratch_shapes=[pltpu.VMEM((2 * blocks, rows, rows), jnp.float32)],
    )(pos, *[k for k, _ in parts], *[r for _, r in parts])[None]


def solution(mesh):
    placed = (P("grp", "row", None), P(), P(), P(), P())
    return jax.shard_map(
        functools.partial(body, mesh.shape["grp"], mesh.shape["row"]),
        mesh=mesh,
        in_specs=placed,
        out_specs=P("grp", "row", None),
        check_vma=False,
    )
```
